32 devices in a mesh: dp: 4 (over z), row: 4 (over y, x), col: 2 (over core).
Axes of the slice: x: 2, y: 2, z: 4, core: 2. Of those that a mesh axis runs over, the one named last changes fastest.
Arguments:
- block_input: bfloat16 [4096, 1024], P(('dp', 'row'), 'col'), may hold values from -20 to 20
- output_grad: bfloat16 [4096, 1024], P(('dp', 'row'), 'col'), may hold values from -6 to 6
- document_ids: int32 [4, 1024], P('dp'), may hold values from 0 to 3, never falling along the last dimension, each value on 1 to 512 neighbouring positions
- mixer_gain: bfloat16 [1024], P('col'), may hold values from 0.25 to 1.75
- mamba_gate: bfloat16 [1024, 1536], P('col', 'row'), may hold values from -0.1875 to 0.1875
- mamba_input: bfloat16 [1024, 1536], P('col', 'row'), may hold values from -0.1875 to 0.1875
- mamba_step: bfloat16 [1024, 24], P('col', 'row'), may hold values from -0.1875 to 0.1875
- query_weight: bfloat16 [1024, 512], P('col', 'row'), may hold values from -0.1875 to 0.1875
- key_weight: bfloat16 [1024, 128], P('col'), may hold values from -0.1875 to 0.1875
- value_weight: bfloat16 [1024, 128], P('col'), may hold values from -0.1875 to 0.1875
- state_weight: bfloat16 [1024, 256], P('col'), may hold values from -0.1875 to 0.1875
- input_filter: bfloat16 [1536, 4], P(('row', 'col')), may hold values from -3 to 3
- input_shift: bfloat16 [1536], P(('row', 'col')), may hold values from -0.5 to 0.5
- state_filter: bfloat16 [256, 4], replicated, may hold values from -3 to 3
- state_shift: bfloat16 [256], replicated, may hold values from -0.5 to 0.5
- step_bias: bfloat16 [24], P(('row', 'col')), may hold values from -5 to -1
- decay_log: bfloat16 [24], P(('row', 'col')), may hold values from 0 to 2.6875
- skip_gain: bfloat16 [24], P(('row', 'col')), may hold values from 0.5 to 1.5
- mixer_out: bfloat16 [2048, 1024], P('row', 'col'), may hold values from -4 to 4
- feed_gain: bfloat16 [1024], P('col'), may hold values from 0.25 to 1.75
- feed_gate: bfloat16 [1024, 2048], P('col', 'row'), may hold values from -0.1875 to 0.1875
- feed_up: bfloat16 [1024, 2048], P('col', 'row'), may hold values from -0.1875 to 0.1875
- feed_down: bfloat16 [2048, 1024], P('row', 'col'), may hold values from -0.125 to 0.125
Outputs:
- block_output: float32 [4096, 1024], P(('dp', 'row'), 'col')
- input_grad: float32 [4096, 1024], P(('dp', 'row'), 'col')
- mixer_gain_gradient: float32 [1024], P('col')
- mamba_gate_gradient: float32 [1024, 1536], P('col', 'row')
- mamba_input_gradient: float32 [1024, 1536], P('col', 'row')
- mamba_step_gradient: float32 [1024, 24], P('col', 'row')
- query_weight_gradient: float32 [1024, 512], P('col', 'row')
- key_weight_gradient: float32 [1024, 128], P('col')
- value_weight_gradient: float32 [1024, 128], P('col')
- state_weight_gradient: float32 [1024, 256], P('col')
- input_filter_gradient: float32 [1536, 4], P(('row', 'col'))
- input_shift_gradient: float32 [1536], P(('row', 'col'))
- state_filter_gradient: float32 [256, 4], replicated
- state_shift_gradient: float32 [256], replicated
- step_bias_gradient: float32 [24], P(('row', 'col'))
- decay_log_gradient: float32 [24], P(('row', 'col'))
- skip_gain_gradient: float32 [24], P(('row', 'col'))
- mixer_out_gradient: float32 [2048, 1024], P('row', 'col')
- feed_gain_gradient: float32 [1024], P('col')
- feed_gate_gradient: float32 [1024, 2048], P('col', 'row')
- feed_up_gradient: float32 [1024, 2048], P('col', 'row')
- feed_down_gradient: float32 [2048, 1024], P('row', 'col')
The draws below stay inside these ranges and needn't reach their ends.
Inputs may be any that keep to these rules, and one draw needn't show every extreme that they name: `document_ids`: along a sequence the document number never falls; each document is a run of one to half of 1024 tokens, and one run in each sequence is exactly that long.
All inputs are finite; a program needn't handle non-finite values.
Results may differ from the reference program's by a relative error of at most 0.039.
Values may be sent and summed in bfloat16 or wider, within the bound.
No kernel may reach another device: no remote copies, remote signals or barrier semaphores. Data moves between devices by JAX's collectives and lax.ppermute only.
A program may use at most 128 MiB of HBM per device.

```python
import math
import jax
import jax.numpy as jnp
import numpy as np
from jax import lax

D = 1024
HM = 24
HD = 64
N = 128
QH = 8
KVH = 2
FF = 2048
KCONV = 4
L = 1024
STRETCH = 256
DOCS = 4
DSSM = 1536
HPD = 3
SEQUENCES = 4
TOKENS = 4096
N_COL = 2


def draw_block_input(key, part):
    keys = jax.random.split(key, 3)
    column = jnp.arange(D).astype(jnp.float32) / D
    column_scale = 0.5 * 3.0 ** column * jax.random.uniform(keys[0], (D,), minval=0.8, maxval=1.25)
    row_scale = jnp.exp(jax.random.uniform(keys[1], (TOKENS, 1), minval=-1.2, maxval=0.5))
    base = jnp.clip(jax.random.normal(keys[2], (TOKENS, D)), -5.0, 5.0)
    return (base * column_scale * row_scale).astype(jnp.bfloat16)


def draw_mixer_out(key, part):
    span = HPD * HD + HD
    index = jnp.arange(DSSM + QH * HD) % span
    scale = jnp.where(index >= HPD * HD, (QH * HD / 64.0) ** (-0.5), DSSM ** (-0.5))
    values = jax.random.normal(key, (DSSM + QH * HD, D)) * scale[:, None]
    return values.astype(jnp.bfloat16)


def block_scale(key, shape, cuts, least, high):
    def one(dim, blocks):
        steps = jax.random.uniform(jax.random.fold_in(jax.random.fold_in(key, 6), dim), (blocks,), jnp.float32, least / len(cuts), high / len(cuts))
        return jnp.repeat(jnp.exp(steps), shape[dim] // blocks).reshape((-1,) + (1,) * (len(shape) - dim - 1))

    factor_of = one(*cuts[0])
    for cut in cuts[1:]:
        factor_of = factor_of * one(*cut)
    return factor_of


def split_up(number_of, total, most, lean):
    loads = [(1 << 20) // math.isqrt(standing ** lean) + 1 for standing in range(2, number_of + 1)]
    rest, counts = total - most - (number_of - 1), [1] * (number_of - 1)
    while rest > 0:
        free = [i for i in range(number_of - 1) if counts[i] < most]
        pool, remaining = sum([loads[i] for i in free]), rest
        for i in free:
            extra = min(most - counts[i], max(1, remaining * loads[i] // pool), rest)
            counts[i] = counts[i] + extra
            rest = rest - extra
    return np.array([most] + counts)


def ragged_sizes(stream_key, count, total, reach, slope):
    if count == 2:
        one = jax.random.randint(stream_key, (), max(1, total - reach), min(reach, total - 1) + 1)
        return jnp.stack([one, total - one])
    lengths = jnp.asarray(split_up(count, total, reach, slope), jnp.int32)
    twos = (count - 1) // 2
    source_of, receiver = lengths[1:1 + 2 * twos:2], lengths[2:2 + 2 * twos:2]
    room = jnp.minimum(source_of - 1, reach - receiver)
    shifted = jax.random.randint(jax.random.fold_in(stream_key, 1), (twos,), 0, 1 << 20) % (room + 1)
    lengths = lengths.at[1:1 + 2 * twos:2].set(source_of - shifted).at[2:2 + 2 * twos:2].set(receiver + shifted)
    return lengths[jax.random.permutation(jax.random.fold_in(stream_key, 2), count)]


def noise(own_key, dims, scale, bound, cuts=(), kind=jnp.bfloat16):
    drawn = scale * jax.random.normal(own_key, dims, jnp.float32)
    if cuts:
        drawn = drawn * block_scale(own_key, dims, cuts, -0.22, 0.18)
    return jnp.clip(drawn, -bound, bound).astype(kind)


def setup_inputs(seed: int = 0) -> dict:
    streams_of = jax.random.split(jax.random.key(seed), 24)
    block_input = draw_block_input(jax.random.fold_in(streams_of[23], 71), 0)
    output_grad = noise(streams_of[1], (TOKENS, D), 1.0, 6.0, ((0, 16), (1, 2)))
    document_ids = jax.vmap(lambda own: jnp.searchsorted(jnp.cumsum(ragged_sizes(own, DOCS, L, L // 2, 2)), jnp.arange(L), side="right"))(jax.random.split(streams_of[2], SEQUENCES)).reshape((SEQUENCES, L)).astype(jnp.int32)
    mixer_gain = jnp.clip(1.0 + 0.15 * jax.random.normal(streams_of[3], (D,), jnp.float32), 0.25, 1.75).astype(jnp.bfloat16)
    mamba_gate = noise(streams_of[4], (D, DSSM), D ** -0.5, 0.1875, ((0, 2), (1, 4)))
    mamba_input = noise(streams_of[5], (D, DSSM), D ** -0.5, 0.1875, ((0, 2), (1, 4)))
    mamba_step = noise(streams_of[6], (D, HM), D ** -0.5, 0.1875, ((0, 2), (1, 4)))
    query_weight = noise(streams_of[7], (D, QH * HD), D ** -0.5, 0.1875, ((0, 2), (1, 4)))
    key_weight = noise(streams_of[8], (D, KVH * HD), D ** -0.5, 0.1875, ((0, 2),))
    value_weight = noise(streams_of[9], (D, KVH * HD), D ** -0.5, 0.1875, ((0, 2),))
    state_weight = noise(streams_of[10], (D, 2 * N), D ** -0.5, 0.1875, ((0, 2),))
    input_filter = noise(streams_of[11], (DSSM, KCONV), KCONV ** -0.5, 3.0, ((0, 8),))
    input_shift = jnp.clip(jax.random.uniform(streams_of[12], (DSSM,), jnp.float32, -0.5, 0.5) * block_scale(streams_of[12], (DSSM,), ((0, 8),), -0.4, 0.0), -0.5, 0.5).astype(jnp.bfloat16)
    state_filter = noise(streams_of[13], (2 * N, KCONV), KCONV ** -0.5, 3.0)
    state_shift = jnp.clip(jax.random.uniform(streams_of[14], (2 * N,), jnp.float32, -0.5, 0.5), -0.5, 0.5).astype(jnp.bfloat16)
    step_bias = jnp.clip(-5.0 + 4.0 * jax.random.uniform(streams_of[15], (HM,), jnp.float32) ** block_scale(streams_of[15], (HM,), ((0, 8),), -0.2, 0.2), -5.0, -1.0).astype(jnp.bfloat16)
    decay_log = jnp.clip(2.6875 * jax.random.uniform(streams_of[16], (HM,), jnp.float32) ** block_scale(streams_of[16], (HM,), ((0, 8),), -0.2, 0.2), 0.0, 2.6875).astype(jnp.bfloat16)
    skip_gain = jnp.clip(0.5 + 1.0 * jax.random.uniform(streams_of[17], (HM,), jnp.float32) ** block_scale(streams_of[17], (HM,), ((0, 8),), -0.2, 0.2), 0.5, 1.5).astype(jnp.bfloat16)
    mixer_out = draw_mixer_out(jax.random.fold_in(streams_of[23], 71), 0)
    feed_gain = jnp.clip(1.0 + 0.15 * jax.random.normal(streams_of[19], (D,), jnp.float32), 0.25, 1.75).astype(jnp.bfloat16)
    feed_gate = noise(streams_of[20], (D, FF), D ** -0.5, 0.1875, ((0, 2), (1, 4)))
    feed_up = noise(streams_of[21], (D, FF), D ** -0.5, 0.1875, ((0, 2), (1, 4)))
    feed_down = noise(streams_of[22], (FF, D), FF ** -0.5, 0.125, ((0, 4), (1, 2)))
    return dict(block_input=block_input, output_grad=output_grad, document_ids=document_ids, mixer_gain=mixer_gain, mamba_gate=mamba_gate, mamba_input=mamba_input, mamba_step=mamba_step, query_weight=query_weight, key_weight=key_weight, value_weight=value_weight, state_weight=state_weight, input_filter=input_filter, input_shift=input_shift, state_filter=state_filter, state_shift=state_shift, step_bias=step_bias, decay_log=decay_log, skip_gain=skip_gain, mixer_out=mixer_out, feed_gain=feed_gain, feed_gate=feed_gate, feed_up=feed_up, feed_down=feed_down)


@jax.custom_vjp
def low(v):
    return lax.optimization_barrier(v.astype(jnp.bfloat16)).astype(jnp.float32)

@jax.custom_vjp
def low_back(v):
    return v

def low_keep(v):
    return (low(v), None)

def low_pass(kept, grad):
    return (grad,)

def back_keep(v):
    return (v, None)

def back_low(kept, grad):
    return (low(grad),)
low.defvjp(low_keep, low_pass)
low_back.defvjp(back_keep, back_low)
EPS = 1e-05
ROPE_BASE = 100000000000.0
HIGH = lax.Precision.HIGHEST

def matmul(left, right):
    return jnp.dot(left, right, precision=HIGH)

def normalize(values, gain):
    return values * lax.rsqrt(lax.optimization_barrier(jnp.mean(values * values, axis=-1, keepdims=True)) + EPS) * gain

def causal_filter(values, weight, shift):
    taps = weight.shape[1]
    length = values.shape[1]
    padded = jnp.pad(values, ((0, 0), (taps - 1, 0), (0, 0)))
    result = shift + padded[:, 0:length] * weight[:, 0]
    for index in range(1, taps):
        result = result + padded[:, index:index + length] * weight[:, index]
    return result

def rotate(values, sign):
    length = values.shape[-3]
    width = values.shape[-1]
    half = width // 2
    place = jnp.arange(length).astype(values.dtype)
    rates = ROPE_BASE ** (-2.0 * jnp.arange(half).astype(values.dtype) / width)
    angle = place[:, None] * rates[None, :]
    cosine = jnp.cos(angle)[:, None, :]
    sine = sign * jnp.sin(angle)[:, None, :]
    first = values[..., :half]
    second = values[..., half:]
    return jnp.concatenate([first * cosine - second * sine, second * cosine + first * sine], axis=-1)

def ssd_scan(inputs, steps, rates, inject, readout, segment):
    length, heads, width = inputs.shape
    states = inject.shape[1]
    blocks = length // STRETCH
    place = jnp.arange(STRETCH)
    before = place[:, None] >= place[None, :]

    def advance(carry, piece):
        state, last_doc = carry
        part_in, part_step, part_inject, part_read, part_doc = piece
        logs = jnp.cumsum(part_step * rates, axis=0)
        allowed = ((part_doc[:, None] == part_doc[None, :]) & before)[:, :, None]
        spread = jnp.where(allowed, logs[:, None, :] - logs[None, :, :], 0.0)
        decay = jnp.where(allowed, jnp.exp(spread), 0.0)
        intersection = jnp.dot(part_read, part_inject.T, precision=HIGH)
        mixing = intersection[:, :, None] * decay * part_step[None, :, :]
        inner = jnp.einsum('tsh,shp->thp', mixing, part_in, precision=HIGH)
        keep = (part_doc == last_doc).astype(part_in.dtype)
        carried = jnp.einsum('tn,hnp->thp', part_read, state, precision=HIGH) * (jnp.exp(logs) * keep[:, None])[:, :, None]
        end_doc = part_doc[STRETCH - 1]
        tail = (part_doc == end_doc).astype(part_in.dtype)
        towards = jnp.exp(logs[STRETCH - 1][None, :] - logs) * tail[:, None] * part_step
        going = jnp.exp(logs[STRETCH - 1]) * (end_doc == last_doc).astype(part_in.dtype)
        state = state * going[:, None, None] + jnp.einsum('sh,sn,shp->hnp', towards, part_inject, part_in, precision=HIGH)
        return ((state, end_doc), inner + carried)

    def split(values):
        return values.reshape((blocks, STRETCH) + values.shape[1:])
    start = (jnp.zeros((heads, states, width), inputs.dtype), jnp.int32(-1))
    final, outputs = lax.scan(jax.checkpoint(advance), start, (split(inputs), split(steps), split(inject), split(readout), split(segment)))
    return outputs.reshape(length, heads, width)

def mamba_piece(segment, input_values, gate_values, step_values, state_conv, filter_weight, filter_shift, step_bias, decay_log, skip_gain):
    sequences, length = segment.shape
    heads = step_values.shape[1]
    channels = input_values.shape[1]
    width = channels // heads
    states = state_conv.shape[1] // 2
    filtered = jax.nn.silu(causal_filter(input_values.reshape(sequences, length, channels), filter_weight, filter_shift))
    filtered = filtered.reshape(sequences, length, heads, width)
    steps = jax.nn.softplus(step_values + step_bias).reshape(sequences, length, heads)
    rates = -jnp.exp(decay_log)
    shared = state_conv.reshape(sequences, length, 2 * states)
    mixed = jax.vmap(ssd_scan, in_axes=(0, 0, None, 0, 0, 0))(filtered, steps, rates, shared[..., :states], shared[..., states:], segment)
    mixed = mixed + skip_gain[:, None] * filtered
    return mixed.reshape(sequences * length, channels) * jax.nn.silu(gate_values)

def block_partials(normed, weight):
    length = normed.shape[0]
    width = normed.shape[1] // N_COL
    parts = jnp.einsum('lcd,cdf->clf', normed.reshape(length, N_COL, width), weight.reshape(N_COL, width, weight.shape[1]), precision=HIGH)
    return lax.optimization_barrier(jnp.sum(low(parts), axis=0))

def attention(query, keys, values, segment):
    group = QH // KVH
    keys_all = jnp.repeat(keys, group, axis=1)
    values_all = jnp.repeat(values, group, axis=1)
    raw = low_back(jnp.einsum('qhd,khd->hqk', query, keys_all, precision=HIGH))
    place = jnp.arange(query.shape[0])
    allowed = (segment[:, None] == segment[None, :]) & (place[:, None] >= place[None, :])
    scores = jnp.where(allowed[None], raw * HD ** (-0.5), -1e+30)
    probs = low(jax.nn.softmax(scores, axis=-1))
    return jnp.einsum('hqk,khd->qhd', probs, values_all, precision=HIGH)

def layer(params, inputs, segment):
    mixer_gain, mamba_gate, mamba_input, mamba_step, query_weight, key_weight, value_weight, state_weight, input_filter, input_shift, state_filter, state_shift, step_bias, decay_log, skip_gain, mixer_out, feed_gain, feed_gate, feed_up, feed_down = params
    length = inputs.shape[0]
    normed = low(normalize(inputs, mixer_gain))
    gate_values = low_back(matmul(normed, mamba_gate))
    input_values = low_back(matmul(normed, mamba_input))
    step_values = low_back(matmul(normed, mamba_step))
    query_pre = low_back(matmul(normed, query_weight))
    state_raw = block_partials(normed, state_weight)
    key_raw = block_partials(normed, key_weight)
    value_raw = block_partials(normed, value_weight)
    state_conv = jax.nn.silu(causal_filter(state_raw[None], state_filter, state_shift))[0]
    gated = mamba_piece(segment[None], input_values, gate_values, step_values, state_conv, input_filter, input_shift, step_bias, decay_log, skip_gain)
    query = low(rotate(query_pre.reshape(length, QH, HD), 1.0))
    keys = low(rotate(key_raw.reshape(length, KVH, HD), 1.0))
    values = low(value_raw.reshape(length, KVH, HD))
    attended = attention(query, keys, values, segment)
    gated_low = low_back(low(gated))
    attended_low = low_back(low(attended.reshape(length, QH * HD)))
    features = jnp.concatenate([gated_low.reshape(length, QH, HPD * HD), attended_low.reshape(length, QH, HD)], axis=2)
    features = features.reshape(length, DSSM + QH * HD)
    after_mixer = inputs + low_back(matmul(features, mixer_out))
    normed_two = low(normalize(after_mixer, feed_gain))
    gate = low_back(matmul(normed_two, feed_gate))
    upper = low_back(matmul(normed_two, feed_up))
    hidden = low_back(low(jax.nn.silu(gate) * upper))
    return after_mixer + low_back(matmul(hidden, feed_down))

def reference(block_input, output_grad, document_ids, mixer_gain, mamba_gate, mamba_input, mamba_step, query_weight, key_weight, value_weight, state_weight, input_filter, input_shift, state_filter, state_shift, step_bias, decay_log, skip_gain, mixer_out, feed_gain, feed_gate, feed_up, feed_down):
    params = tuple((item.astype(jnp.float32) for item in (mixer_gain, mamba_gate, mamba_input, mamba_step, query_weight, key_weight, value_weight, state_weight, input_filter, input_shift, state_filter, state_shift, step_bias, decay_log, skip_gain, mixer_out, feed_gain, feed_gate, feed_up, feed_down)))
    inputs = block_input.astype(jnp.float32).reshape(-1, L, D)
    cotangent = output_grad.astype(jnp.float32).reshape(-1, L, D)

    def one(carry, item):
        sequence, upstream, segment = item

        def apply(weights, values):
            return layer(weights, values, segment)
        output, pull = jax.vjp(apply, params, sequence)
        weight_grads, input_part = pull(upstream)
        return (jax.tree.map(jnp.add, carry, weight_grads), (output, input_part))
    zeros = jax.tree.map(jnp.zeros_like, params)
    total, (outputs, input_parts) = lax.scan(one, zeros, (inputs, cotangent, document_ids))
    return (outputs.reshape(-1, D), input_parts.reshape(-1, D), total[0], total[1], total[2], total[3], total[4], total[5], total[6], total[7], total[8], total[9], total[10], total[11], total[12], total[13], total[14], total[15], total[16], total[17], total[18], total[19])
```

```python
import jax
import jax.numpy as jnp
from jax import lax
from jax.experimental import pallas as pl
from jax.experimental.pallas import tpu as pltpu
from jax.sharding import PartitionSpec as P

D = 1024
HD = 64
QH = 8
KVH = 2
NS = 128
HPD = 3

EPS = 1e-05
ROPE_BASE = 100000000000.0
HIGH = lax.Precision.HIGHEST
BF = jnp.bfloat16
F32 = jnp.float32

SX = 2 * NS
SQ = SX + HPD * HD
SZ = SQ + HD
SS = SZ + HPD * HD
SK = SS + HD
SV = SK + HD
WIDE = SV + HD


def dg(left, right, ca, cb, precision=None):
    return lax.dot_general(
        left, right, (((ca,), (cb,)), ((), ())), precision=precision, preferred_element_type=F32
    )


def product(left, right):
    return dg(left, right, 1, 0)


def against(left, right):
    return dg(left, right, 1, 1)


def outer(left, right):
    return dg(left, right, 0, 0)


def swap(value):
    return lax.ppermute(value, "col", [(0, 1), (1, 0)])


def flip(value, axis, step):
    count = lax.axis_size(axis)
    return lax.ppermute(value, axis, [(i, i ^ step) for i in range(count)])


def rope(value, cosine, sine):
    half = HD // 2
    turned = jnp.concatenate([-value[:, half:], value[:, :half]], axis=1)
    return value * cosine + turned * sine


def unrope(value, cosine, sine):
    half = HD // 2
    turned = jnp.concatenate([value[:, half:], -value[:, :half]], axis=1)
    return value * cosine + turned * sine


def spread(cols, width):
    rows = cols[0].shape[0]
    return jnp.concatenate([jnp.broadcast_to(c, (rows, width)) for c in cols], axis=1)


def head_sums(value):
    return [jnp.sum(value[:, h * HD : (h + 1) * HD], axis=1, keepdims=True) for h in range(HPD)]


def load_tokens(r, parts, whole, rows):
    whole[0:8, :] = jnp.zeros((8, whole.shape[1]), F32)
    for k in range(len(parts)):
        start = pl.multiple_of((r ^ k) * rows + 8, 8)
        whole[pl.ds(start, rows), :] = parts[k][...]


def filtered(whole, taps, first, rows):
    pre = taps[4:5, :] + whole[pl.ds(first + 5, rows), 0:SZ] * taps[0:1, :]
    for j in range(1, 4):
        pre = pre + whole[pl.ds(first + 5 + j, rows), 0:SZ] * taps[j : j + 1, :]
    return pre


def step_parts(whole, heads, first, rows, tri):
    raw = whole[pl.ds(first + 8, rows), SS:SK] + heads[0:1, :]
    step = jnp.maximum(raw, 0.0) + jnp.log1p(jnp.exp(-jnp.abs(raw)))
    logs = dg(tri, step * heads[1:2, :], 1, 0, HIGH)
    turned = jnp.transpose(jnp.concatenate([step, logs], axis=1))
    return raw, step, logs, turned


def masks(doc_col, doc_row, first, last, rows):
    dc = doc_col[pl.ds(first, rows), :]
    t = lax.broadcasted_iota(jnp.int32, (rows, last), 0) + first
    s = lax.broadcasted_iota(jnp.int32, (rows, last), 1)
    return (dc == doc_row[:, 0:last]) & (t >= s)


def forward_kernel(
    r_ref, p0, p1, p2, p3, cosine, sine, doc_col, doc_row, taps, heads, skip,
    feat, total, states, lse, whole, qs, ks, vs, state,
):
    r = r_ref[0]
    rows = p0.shape[0]
    chunks = 4
    load_tokens(r, (p0, p1, p2, p3), whole, rows)
    ti = lax.broadcasted_iota(jnp.int32, (rows, rows), 0)
    si = lax.broadcasted_iota(jnp.int32, (rows, rows), 1)
    tri = (ti >= si).astype(F32)
    state[...] = jnp.zeros_like(state)
    scale = HD ** (-0.5)
    for c in range(chunks):
        first = c * rows
        slot = r ^ c
        pre = filtered(whole, taps[...], first, rows)
        act = pre * jax.nn.sigmoid(pre)
        inject = act[:, 0:NS].astype(BF)
        read = act[:, NS : 2 * NS].astype(BF)
        inner_x = act[:, SX:SQ]
        raw, step, logs, turned = step_parts(whole, heads[...], first, rows, tri)
        dc = doc_col[pl.ds(first, rows), :]
        allowed = (dc == doc_row[:, first : first + rows]) & (ti >= si)
        dt = spread([step[:, h : h + 1] for h in range(HPD)], HD)
        lg = spread([logs[:, h : h + 1] for h in range(HPD)], HD)
        xd = (inner_x * dt).astype(BF)
        meet = against(read, inject)
        inner = []
        for h in range(HPD):
            gap = logs[:, h : h + 1] - turned[HD + h : HD + h + 1, :]
            decay = jnp.exp(jnp.where(allowed, gap, -1e30))
            inner.append(product((meet * decay).astype(BF), xd[:, h * HD : (h + 1) * HD]))
        inner = jnp.concatenate(inner, axis=1)
        old = state[...]
        states[c] = old
        end_doc = dc[rows - 1 : rows, :]
        last_doc = doc_col[first - 1 : first, :] if c else end_doc - 1
        keep = (dc == last_doc).astype(F32)
        carried = product(read, old.astype(BF)) * (jnp.exp(lg) * keep)
        tail = (dc == end_doc).astype(F32)
        end = lg[rows - 1 : rows, :]
        toward = jnp.exp(end - lg) * tail * dt
        going = jnp.exp(end) * (end_doc == last_doc).astype(F32)
        state[...] = old * going + outer(inject, (toward * inner_x).astype(BF))
        y = inner + carried + skip[...] * inner_x
        total[pl.ds(first, rows), :] = y
        z = whole[pl.ds(first + 8, rows), SZ:SS]
        gated = y * (z * jax.nn.sigmoid(z))
        cs = cosine[pl.ds(first, rows), :]
        sn = sine[pl.ds(first, rows), :]
        query = rope(whole[pl.ds(first + 8, rows), SQ:SZ], cs, sn).astype(BF)
        qs[pl.ds(first, rows), :] = query
        ks[pl.ds(first, rows), :] = rope(whole[pl.ds(first + 8, rows), SK:SV], cs, sn).astype(BF)
        vs[pl.ds(first, rows), :] = whole[pl.ds(first + 8, rows), SV:WIDE].astype(BF)
        last = first + rows
        score = jnp.where(
            masks(doc_col, doc_row, first, last, rows),
            against(query, ks[0:last, :]) * scale,
            -1e30,
        )
        peak = jnp.max(score, axis=1, keepdims=True)
        weight = jnp.exp(score - peak)
        bottom = jnp.sum(weight, axis=1, keepdims=True)
        att = product((weight / bottom).astype(BF), vs[0:last, :])
        lse[pl.ds(first, rows), :] = peak + jnp.log(bottom)
        feat[slot] = jnp.concatenate([gated, att], axis=1).astype(BF)


def backward_kernel(
    r_ref, p0, p1, p2, p3, dfeat, total, states, lse, cosine, sine, doc_col, doc_row, taps,
    heads, skip, dproj, small, whole, dpre, qs, ks, vs, dks, dvs, dstate,
):
    r = r_ref[0]
    rows = p0.shape[0]
    chunks = 4
    load_tokens(r, (p0, p1, p2, p3), whole, rows)
    ti = lax.broadcasted_iota(jnp.int32, (rows, rows), 0)
    si = lax.broadcasted_iota(jnp.int32, (rows, rows), 1)
    tri = (ti >= si).astype(F32)
    scale = HD ** (-0.5)
    small[...] = jnp.zeros_like(small)
    dstate[...] = jnp.zeros_like(dstate)
    dks[...] = jnp.zeros_like(dks)
    dvs[...] = jnp.zeros_like(dvs)
    dpre[chunks * rows :, :] = jnp.zeros((8, SZ), F32)
    for c in range(chunks):
        first = c * rows
        cs = cosine[pl.ds(first, rows), :]
        sn = sine[pl.ds(first, rows), :]
        qs[pl.ds(first, rows), :] = rope(whole[pl.ds(first + 8, rows), SQ:SZ], cs, sn).astype(BF)
        ks[pl.ds(first, rows), :] = rope(whole[pl.ds(first + 8, rows), SK:SV], cs, sn).astype(BF)
        vs[pl.ds(first, rows), :] = whole[pl.ds(first + 8, rows), SV:WIDE].astype(BF)
    for c in reversed(range(chunks)):
        first = c * rows
        last = first + rows
        slot = r ^ c
        datt = dfeat[slot, :, HPD * HD :]
        query = qs[pl.ds(first, rows), :]
        score = jnp.where(
            masks(doc_col, doc_row, first, last, rows),
            against(query, ks[0:last, :]) * scale,
            -1e30,
        )
        prob = jnp.exp(score - lse[pl.ds(first, rows), :])
        dprob = against(datt, vs[0:last, :])
        lean = jnp.sum(prob * dprob, axis=1, keepdims=True)
        dscore = (prob * (dprob - lean) * scale).astype(BF)
        dq = product(dscore, ks[0:last, :])
        dks[0:last, :] += outer(dscore, query)
        dvs[0:last, :] += outer(prob.astype(BF), datt)
        cs = cosine[pl.ds(first, rows), :]
        sn = sine[pl.ds(first, rows), :]
        dproj[slot, :, SQ:SZ] = unrope(dq, cs, sn).astype(BF)
        dproj[slot, :, SK:WIDE] = jnp.concatenate(
            [unrope(dks[pl.ds(first, rows), :], cs, sn), dvs[pl.ds(first, rows), :]], axis=1
        ).astype(BF)

        pre = filtered(whole, taps[...], first, rows)
        sig = jax.nn.sigmoid(pre)
        act = pre * sig
        inject = act[:, 0:NS].astype(BF)
        read = act[:, NS : 2 * NS].astype(BF)
        inner_x = act[:, SX:SQ]
        raw, step, logs, turned = step_parts(whole, heads[...], first, rows, tri)
        dc = doc_col[pl.ds(first, rows), :]
        allowed = (dc == doc_row[:, first:last]) & (ti >= si)
        dt = spread([step[:, h : h + 1] for h in range(HPD)], HD)
        lg = spread([logs[:, h : h + 1] for h in range(HPD)], HD)
        end_doc = dc[rows - 1 : rows, :]
        last_doc = doc_col[first - 1 : first, :] if c else end_doc - 1
        keep = (dc == last_doc).astype(F32)
        tail = (dc == end_doc).astype(F32)
        end = lg[rows - 1 : rows, :]
        going = jnp.exp(end) * (end_doc == last_doc).astype(F32)
        near = jnp.exp(end - lg) * tail
        toward = near * dt
        ek = jnp.exp(lg) * keep

        dgated = dfeat[slot, :, 0 : HPD * HD].astype(F32)
        z = whole[pl.ds(first + 8, rows), SZ:SS]
        zs = jax.nn.sigmoid(z)
        dz = dgated * total[pl.ds(first, rows), :] * (zs * (1.0 + z * (1.0 - zs)))
        dy = dgated * (z * zs)
        dyb = dy.astype(BF)
        small[6:7, 0 : HPD * HD] += jnp.sum(dy * inner_x, axis=0, keepdims=True)
        xd = (inner_x * dt).astype(BF)
        old = states[c]
        oldb = old.astype(BF)
        dst = dstate[...]
        dstb = dst.astype(BF)
        meet = against(read, inject)
        dmeet = jnp.zeros((rows, rows), F32)
        ahead = []
        behind = []
        dxt = []
        for h in range(HPD):
            gap = logs[:, h : h + 1] - turned[HD + h : HD + h + 1, :]
            decay = jnp.exp(jnp.where(allowed, gap, -1e30))
            mixed = meet * decay
            dyh = dyb[:, h * HD : (h + 1) * HD]
            dxt.append(outer(mixed.astype(BF), dyh))
            dmix = against(dyh, xd[:, h * HD : (h + 1) * HD])
            dmeet = dmeet + dmix * decay
            flow = dmix * mixed
            ahead.append(jnp.sum(flow, axis=1, keepdims=True))
            behind.append(jnp.sum(flow, axis=0, keepdims=True))
        dxt = jnp.concatenate(dxt, axis=1)
        behind = jnp.transpose(
            jnp.concatenate(behind + [jnp.zeros((128 - HPD, rows), F32)], axis=0)
        )
        v = product(inject, dstb)
        dx = skip[...] * dy + dt * dxt + toward * v
        pull = head_sums(inner_x * dxt)
        xv = inner_x * v
        push = head_sums(near * xv)
        send = toward * xv
        sends = head_sums(send)
        seen = head_sums(dy * (product(read, oldb) * ek))
        dyk = (dy * ek).astype(BF)
        dmeet = dmeet.astype(BF)
        dread = product(dmeet, inject) + against(dyk, oldb)
        dinject = outer(dmeet, read) + against((toward * inner_x).astype(BF), dstb)
        closing = jnp.sum(send, axis=0, keepdims=True) + jnp.sum(
            dst * old, axis=0, keepdims=True
        ) * going
        closing = head_sums(closing)
        dstate[...] = dst * going + outer(read, dyk)
        dlog = jnp.concatenate(
            [ahead[h] + seen[h] - sends[h] - behind[:, h : h + 1] for h in range(HPD)]
            + [jnp.zeros((rows, HD - HPD), F32)],
            axis=1,
        )
        ends = jnp.concatenate(closing + [jnp.zeros((1, HD - HPD), F32)], axis=1)
        dla = dg(tri, dlog, 0, 0, HIGH) + ends
        dstep = (
            jnp.concatenate(
                [pull[h] + push[h] for h in range(HPD)] + [jnp.zeros((rows, HD - HPD), F32)],
                axis=1,
            )
            + dla * heads[1:2, :]
        )
        draw = dstep * jax.nn.sigmoid(raw)
        lane = lax.broadcasted_iota(jnp.int32, (rows, HD), 1)
        draw = jnp.where(lane < HPD, draw, 0.0)
        small[5:6, 0:HD] += jnp.sum(draw, axis=0, keepdims=True)
        small[5:6, 128 : 128 + HD] += jnp.sum(dla * step, axis=0, keepdims=True) * heads[1:2, :]
        dproj[slot, :, SZ:SK] = jnp.concatenate([dz, draw], axis=1).astype(BF)
        dact = jnp.concatenate([dinject, dread, dx, jnp.zeros((rows, HD), F32)], axis=1)
        dpre[pl.ds(first, rows), :] = dact * (sig * (1.0 + pre * (1.0 - sig)))
    for c in range(chunks):
        first = c * rows
        slot = r ^ c
        here = dpre[pl.ds(first, rows), :]
        back = here * taps[3:4, :]
        small[4:5, :] += jnp.sum(here, axis=0, keepdims=True)
        for j in range(4):
            small[j : j + 1, :] += jnp.sum(
                here * whole[pl.ds(first + 5 + j, rows), 0:SZ], axis=0, keepdims=True
            )
            if j < 3:
                back = back + dpre[pl.ds(first + 3 - j, rows), :] * taps[j : j + 1, :]
        dproj[slot, :, 0:SQ] = back[:, 0:SQ].astype(BF)


def mix_forward(r, parts, tables):
    rows = parts[0].shape[0]
    length = 4 * rows
    vm = pl.BlockSpec(memory_space=pltpu.VMEM)
    return pl.pallas_call(
        forward_kernel,
        name="mix_forward",
        in_specs=[pl.BlockSpec(memory_space=pltpu.SMEM)] + [vm] * 11,
        out_specs=[vm] * 4,
        out_shape=[
            jax.ShapeDtypeStruct((4, rows, HPD * HD + HD), BF),
            jax.ShapeDtypeStruct((length, HPD * HD), F32),
            jax.ShapeDtypeStruct((4, NS, HPD * HD), F32),
            jax.ShapeDtypeStruct((length, 1), F32),
        ],
        scratch_shapes=[
            pltpu.VMEM((length + 8, WIDE), F32),
            pltpu.VMEM((length, HD), BF),
            pltpu.VMEM((length, HD), BF),
            pltpu.VMEM((length, HD), BF),
            pltpu.VMEM((NS, HPD * HD), F32),
        ],
        cost_estimate=pl.CostEstimate(
            flops=2 * 10**9, bytes_accessed=6 * 10**6, transcendentals=2 * 10**6
        ),
        compiler_params=pltpu.CompilerParams(vmem_limit_bytes=60 * 2**20),
    )(r, *parts, *tables)


def mix_backward(r, parts, dfeat, total, states, lse, tables):
    rows = parts[0].shape[0]
    length = 4 * rows
    vm = pl.BlockSpec(memory_space=pltpu.VMEM)
    return pl.pallas_call(
        backward_kernel,
        name="mix_backward",
        in_specs=[pl.BlockSpec(memory_space=pltpu.SMEM)] + [vm] * 15,
        out_specs=[vm] * 2,
        out_shape=[
            jax.ShapeDtypeStruct((4, rows, WIDE), BF),
            jax.ShapeDtypeStruct((8, SZ), F32),
        ],
        scratch_shapes=[
            pltpu.VMEM((length + 8, WIDE), F32),
            pltpu.VMEM((length + 8, SZ), F32),
            pltpu.VMEM((length, HD), BF),
            pltpu.VMEM((length, HD), BF),
            pltpu.VMEM((length, HD), BF),
            pltpu.VMEM((length, HD), F32),
            pltpu.VMEM((length, HD), F32),
            pltpu.VMEM((NS, HPD * HD), F32),
        ],
        cost_estimate=pl.CostEstimate(
            flops=5 * 10**9, bytes_accessed=9 * 10**6, transcendentals=2 * 10**6
        ),
        compiler_params=pltpu.CompilerParams(vmem_limit_bytes=60 * 2**20),
    )(r, *parts, dfeat, total, states, lse, *tables)


def row_spread(block):
    return [block] + [flip(block, "row", k) for k in range(1, 4)]


def row_sum(parts):
    held = parts[0]
    for k in (3, 1, 2):
        held = held + flip(parts[k].astype(BF), "row", k).astype(F32)
    return held


def tree_sum(value, axis):
    step = 1
    while step < lax.axis_size(axis):
        value = value + flip(value, axis, step)
        step *= 2
    return value


def dp_sum(value):
    count = lax.axis_size("dp")
    me = lax.axis_index("dp")
    steps = []
    step = 1
    while step < count:
        steps.append(step)
        step *= 2
    for step in steps:
        half = value.shape[0] // 2
        high = ((me // step) % 2).astype(jnp.int32)
        keep = lax.dynamic_slice_in_dim(value, high * half, half, 0)
        give = lax.dynamic_slice_in_dim(value, (1 - high) * half, half, 0)
        value = (keep.astype(F32) + flip(give, "dp", step).astype(F32)).astype(BF)
    for step in reversed(steps):
        high = (me // step) % 2
        got = flip(value, "dp", step)
        value = jnp.where(
            high == 0,
            jnp.concatenate([value, got], axis=0),
            jnp.concatenate([got, value], axis=0),
        )
    return value


def on_device(
    block_input,
    output_grad,
    document_ids,
    mixer_gain,
    mamba_gate,
    mamba_input,
    mamba_step,
    query_weight,
    key_weight,
    value_weight,
    state_weight,
    input_filter,
    input_shift,
    state_filter,
    state_shift,
    step_bias,
    decay_log,
    skip_gain,
    mixer_out,
    feed_gain,
    feed_gate,
    feed_up,
    feed_down,
):
    length = document_ids.shape[1]
    row = lax.axis_index("row")
    col = lax.axis_index("col")
    pair_head = (row * lax.axis_size("col") + col) // (QH // KVH)
    r = jnp.reshape(row, (1,)).astype(jnp.int32)
    mixer_scale = mixer_gain.astype(F32)
    feed_scale = feed_gain.astype(F32)

    def mine(weight, which, axis):
        half = weight.shape[axis] // 2
        return lax.dynamic_slice_in_dim(weight, which * half, half, axis)

    def joint(which):
        step = mine(mamba_step, which, 1)
        return jnp.concatenate(
            [
                state_weight,
                mine(mamba_input, which, 1),
                mine(query_weight, which, 1),
                mine(mamba_gate, which, 1),
                jnp.pad(step, ((0, 0), (0, HD - step.shape[1]))),
                lax.dynamic_slice_in_dim(key_weight, pair_head * HD, HD, 1),
                lax.dynamic_slice_in_dim(value_weight, pair_head * HD, HD, 1),
            ],
            axis=1,
        )

    residual = block_input.astype(F32)
    square = jnp.sum(residual * residual, axis=1)
    inverse_one = lax.rsqrt((square + swap(square)) / D + EPS)[:, None]
    normed_one = (residual * inverse_one * mixer_scale).astype(BF)
    ones = row_spread(normed_one)
    joint_own = joint(col)
    joint_send = joint(1 - col)
    joint_got = swap(joint_send)
    feed_own = jnp.concatenate([mine(feed_gate, col, 1), mine(feed_up, col, 1)], axis=1)
    feed_send = jnp.concatenate([mine(feed_gate, 1 - col, 1), mine(feed_up, 1 - col, 1)], axis=1)
    feed_got = swap(feed_send)
    parts = []
    for k in range(4):
        parts.append(product(ones[k], joint_own) + product(swap(ones[k]), joint_got))

    half = HD // 2
    place = jnp.arange(length).astype(F32)
    rates = ROPE_BASE ** (-2.0 * jnp.arange(half).astype(F32) / HD)
    angle = place[:, None] * rates[None, :]
    cosine = jnp.concatenate([jnp.cos(angle)] * 2, axis=1)
    sine = jnp.concatenate([jnp.sin(angle)] * 2, axis=1)
    taps = jnp.concatenate(
        [
            jnp.concatenate([state_filter, state_shift[:, None]], axis=1),
            jnp.concatenate([input_filter, input_shift[:, None]], axis=1),
            jnp.zeros((HD, 5), BF),
        ],
        axis=0,
    ).astype(F32).T
    taps = jnp.pad(taps, ((0, 3), (0, 0)))
    heads = jnp.pad(
        jnp.stack([step_bias.astype(F32), -jnp.exp(decay_log.astype(F32))]),
        ((0, 6), (0, HD - HPD)),
    )
    skip = jnp.repeat(skip_gain.astype(F32), HD)[None, :]
    tables = (
        cosine,
        sine,
        document_ids.reshape(length, 1),
        document_ids.reshape(1, length),
        taps,
        heads,
        skip,
    )
    feat, total, states, lse = mix_forward(r, parts, tables)
    feat_got = swap(feat)
    grads = row_spread(output_grad)

    out_own = mine(mixer_out, col, 0)
    out_other = mine(mixer_out, 1 - col, 0)
    after_mixer = residual + row_sum(
        [product(feat[k], out_own) + product(feat_got[k], out_other) for k in range(4)]
    )
    square = jnp.sum(after_mixer * after_mixer, axis=1)
    inverse_two = lax.rsqrt((square + swap(square)) / D + EPS)[:, None]
    normed_two = (after_mixer * inverse_two * feed_scale).astype(BF)
    twos = row_spread(normed_two)

    down_own = mine(feed_down, col, 0)
    down_other = mine(feed_down, 1 - col, 0)
    wide = feed_own.shape[1] // 2
    hidden = []
    edges = []
    hidden_got = []
    edges_got = []
    backs = []
    for k in range(4):
        both = product(twos[k], feed_own) + product(swap(twos[k]), feed_got)
        gate = both[:, :wide]
        upper = both[:, wide:]
        sigma = jax.nn.sigmoid(gate)
        hidden.append((gate * sigma * upper).astype(BF))
        given = against(grads[k], down_own) + swap(against(grads[k], down_other).astype(BF)).astype(
            F32
        )
        edge = jnp.concatenate(
            [
                given * upper * (sigma * (1.0 + gate * (1.0 - sigma))),
                given * (gate * sigma),
            ],
            axis=1,
        ).astype(BF)
        got = swap(edge)
        edges.append(edge)
        edges_got.append(got)
        backs.append(against(edge, feed_own) + against(got, feed_send))
    feed_back = row_sum(backs)
    scaled = feed_back * feed_scale
    inner = jnp.sum(scaled * after_mixer, axis=1)
    inner = (inner + swap(inner))[:, None]
    feed_gain_grad = jnp.sum(feed_back * after_mixer * inverse_two, axis=0)
    mixer_grad = (
        output_grad.astype(F32)
        + inverse_two * scaled
        - after_mixer * (inverse_two**3 * inner / D)
    )
    mixer_low = mixer_grad.astype(BF)
    lows = row_spread(mixer_low)
    dfeat = jnp.stack(
        [
            (
                against(low, out_own) + swap(against(low, out_other).astype(BF)).astype(F32)
            ).astype(BF)
            for low in lows
        ]
    )

    hidden_got = [swap(h) for h in hidden]
    block_output = after_mixer + row_sum(
        [product(hidden[k], down_own) + product(hidden_got[k], down_other) for k in range(4)]
    )
    twos_all = jnp.concatenate(twos, axis=0)
    grads_all = jnp.concatenate(grads, axis=0)
    feed_wgrad = jnp.concatenate(
        [
            outer(twos_all, jnp.concatenate(edges, axis=0)),
            outer(twos_all, jnp.concatenate(edges_got, axis=0)),
            jnp.concatenate(
                [
                    outer(jnp.concatenate(hidden, axis=0), grads_all),
                    outer(jnp.concatenate(hidden_got, axis=0), grads_all),
                ],
                axis=0,
            ),
        ],
        axis=1,
    ).astype(BF)
    feed_sum = dp_sum(feed_wgrad).astype(F32)

    def ordered(own, got, axis):
        return jnp.where(
            col == 0,
            jnp.concatenate([own, got], axis=axis),
            jnp.concatenate([got, own], axis=axis),
        )

    gate_wgrad = ordered(feed_sum[:, 0:wide], feed_sum[:, 2 * wide : 3 * wide], 1)
    upper_wgrad = ordered(feed_sum[:, wide : 2 * wide], feed_sum[:, 3 * wide : 4 * wide], 1)
    down_sum = feed_sum[:, 4 * wide :]
    down_half = down_sum.shape[0] // 2
    down_wgrad = ordered(down_sum[:down_half], down_sum[down_half:], 0)

    lows_all = jnp.concatenate(lows, axis=0)
    flat = feat.shape[2]
    out_sum = dp_sum(
        jnp.concatenate(
            [
                outer(feat.reshape(length, flat), lows_all),
                outer(feat_got.reshape(length, flat), lows_all),
            ],
            axis=0,
        ).astype(BF)
    ).astype(F32)
    out_wgrad = ordered(out_sum[:flat], out_sum[flat:], 0)

    dproj, small = mix_backward(r, parts, dfeat, total, states, lse, tables)
    dproj_got = swap(dproj)
    mixer_back = row_sum(
        [against(dproj[k], joint_own) + against(dproj_got[k], joint_send) for k in range(4)]
    )
    scaled = mixer_back * mixer_scale
    inner = jnp.sum(scaled * residual, axis=1)
    inner = (inner + swap(inner))[:, None]
    mixer_gain_grad = jnp.sum(mixer_back * residual * inverse_one, axis=0)
    input_grad = mixer_grad + (
        inverse_one * scaled - residual * (inverse_one**3 * inner / D)
    )

    ones_all = jnp.concatenate(ones, axis=0)
    own_wgrad = outer(ones_all, dproj.reshape(length, WIDE))
    got_wgrad = outer(ones_all, dproj_got.reshape(length, WIDE))
    mix_sum = dp_sum(
        jnp.concatenate([own_wgrad[:, SX:SK], got_wgrad[:, SX:SK]], axis=1).astype(BF)
    ).astype(F32)
    span = SK - SX

    def pick(start, stop):
        return ordered(
            mix_sum[:, start - SX : stop - SX],
            mix_sum[:, span + start - SX : span + stop - SX],
            1,
        )

    shared = own_wgrad + got_wgrad
    pair = shared[:, SK:WIDE]
    blank = jnp.zeros_like(pair)
    shared = jnp.concatenate(
        [
            shared[:, 0:SX],
            jnp.where(pair_head == 0, pair, blank),
            jnp.where(pair_head == 1, pair, blank),
        ],
        axis=1,
    ).astype(BF)
    deep = shared.shape[0] // 4
    shared = row_sum(
        [
            lax.dynamic_slice_in_dim(shared, (row ^ k) * deep, deep, 0).astype(F32)
            for k in range(4)
        ]
    ).astype(BF)
    shared = dp_sum(shared)
    pieces = row_spread(shared)
    shared = jnp.zeros((4 * deep, shared.shape[1]), BF)
    for k in range(4):
        shared = lax.dynamic_update_slice_in_dim(shared, pieces[k], (row ^ k) * deep, 0)
    shared = shared.astype(F32)
    state_wgrad = shared[:, 0:SX]
    key_wgrad = jnp.concatenate(
        [shared[:, SX : SX + HD], shared[:, SX + 2 * HD : SX + 3 * HD]], axis=1
    )
    value_wgrad = jnp.concatenate(
        [shared[:, SX + HD : SX + 2 * HD], shared[:, SX + 3 * HD : SX + 4 * HD]], axis=1
    )

    small = tree_sum(small, "dp")
    filters = small[0:5, :]
    wide_small = jnp.concatenate(
        [
            jnp.pad(filters[:, 0:SX], ((0, 0), (0, D // 2 - SX))),
            jnp.zeros((3, D // 2), F32),
        ],
        axis=0,
    )
    wide_small = wide_small + swap(wide_small)
    gains = tree_sum(jnp.stack([mixer_gain_grad, feed_gain_grad]), "dp")
    wide_small = tree_sum(jnp.concatenate([wide_small[0:6], gains], axis=0), "row")
    state_filters = wide_small[0:5, 0:SX]
    input_filters = filters[:, SX:SQ]
    skip_wgrad = jnp.sum(small[6, 0 : HPD * HD].reshape(HPD, HD), axis=1)
    return (
        block_output,
        input_grad,
        wide_small[6],
        pick(SZ, SS),
        pick(SX, SQ),
        pick(SS, SS + HPD),
        pick(SQ, SZ),
        key_wgrad,
        value_wgrad,
        state_wgrad,
        input_filters[0:4].T,
        input_filters[4],
        state_filters[0:4].T,
        state_filters[4],
        small[5, 0:HPD],
        small[5, 128 : 128 + HPD],
        skip_wgrad,
        out_wgrad,
        wide_small[7],
        gate_wgrad,
        upper_wgrad,
        down_wgrad,
    )


def solution(mesh):
    tokens = P(("dp", "row"), "col")
    heads = P(("row", "col"))
    placed = (
        tokens,
        tokens,
        P("dp", None),
        P("col"),
        P("col", "row"),
        P("col", "row"),
        P("col", "row"),
        P("col", "row"),
        P("col", None),
        P("col", None),
        P("col", None),
        P(("row", "col"), None),
        heads,
        P(),
        P(),
        heads,
        heads,
        heads,
        P("row", "col"),
        P("col"),
        P("col", "row"),
        P("col", "row"),
        P("row", "col"),
    )
    return jax.shard_map(
        on_device,
        mesh=mesh,
        in_specs=placed,
        out_specs=(
            tokens,
            tokens,
            P("col"),
            P("col", "row"),
            P("col", "row"),
            P("col", "row"),
            P("col", "row"),
            P("col", None),
            P("col", None),
            P("col", None),
            P(("row", "col"), None),
            heads,
            P(),
            P(),
            heads,
            heads,
            heads,
            P("row", "col"),
            P("col"),
            P("col", "row"),
            P("col", "row"),
            P("row", "col"),
        ),
        check_vma=False,
    )
```
